512 devices in a mesh: win: 8 (over z_hi, core), slab: 64 (over z_lo, x, y).
Axes of the slice: x: 4, y: 8, z: 8 (z_hi: 4, z_lo: 2; z = z_hi * 2 + z_lo), core: 2. Of those that a mesh axis runs over, the one named last changes fastest.
Arguments:
- states: float32 [8, 6, 128, 64, 256], P('win', None, 'slab'), may hold values from -6 to 6
- load_shape: bfloat16 [3, 128, 64, 256], P(None, 'slab'), may hold values from -6 to 6
- zone_ids: int32 [128, 64, 256], P('slab'), may hold values from 0 to 7
- zone_shear: float32 [8], replicated, may hold values from 0.3 to 1.2
- zone_lame: float32 [8], replicated, may hold values from 0.3 to 1.5
- amp_table: float32 [16], replicated, may hold values from 0.5 to 2
- cycle_index: int32 [16], replicated, may hold values from 0 to 15, each once
Outputs:
- new_ends: float32 [8, 6, 128, 64, 256], P('win', None, 'slab')
The draws below stay inside these ranges and needn't reach their ends.
Inputs may be any that keep to these rules, and one draw needn't show every extreme that they name: cycle_index holds each of 0 to 15 once.
All inputs are finite; a program needn't handle non-finite values.
Results may differ from the reference program's by a relative error of at most 0.0003.
Values sent between devices are 32-bit elements; how exact they have to be, the bound alone decides.
A program may use at most 64 MiB of HBM per device.

```python
import math
import jax
import jax.numpy as jnp
from jax import lax

NY = 64
NX = 256
FINE = 4
COARSE = 2
ZONES = 8
CYCLES = 16
WINDOWS = 8
NZ = 128


def place_ends(entries, stream_key, least, largest):
    longest = entries.shape.index(max(entries.shape))
    spots = []
    for shift in (0, 1):
        where = [jax.random.randint(jax.random.fold_in(stream_key, axis), (), 0, length) for axis, length in enumerate(entries.shape)]
        where[longest] = (where[longest] + shift) % entries.shape[longest]
        spots.append(tuple(where))
    return entries.at[spots[0]].set(least).at[spots[1]].set(largest)


def steps_of(key, shape, cuts, smallest, high):
    gain = 1.0
    for dim, blocks in cuts:
        draws = jax.random.uniform(jax.random.fold_in(jax.random.fold_in(key, 6), dim), (blocks,), jnp.float32, smallest / len(cuts), high / len(cuts))
        gain = gain * jnp.repeat(jnp.exp(draws), shape[dim] // blocks).reshape((-1,) + (1,) * (len(shape) - 1 - dim))
    return gain


def centred(rng, shape, spread, limit, pieces=(), dtype=jnp.bfloat16):
    drawn = spread * jax.random.normal(rng, shape, jnp.float32)
    if pieces:
        drawn = drawn * steps_of(rng, shape, pieces, -0.22, 0.18)
    return jnp.clip(drawn, -limit, limit).astype(dtype)


def setup_inputs(seed: int = 0) -> dict:
    key_list = jax.random.split(jax.random.key(seed), 8)
    return {
        "states": centred(key_list[0], (WINDOWS, 6, NZ, NY, NX), 1.0, 6.0, ((0, 8), (2, 64)), jnp.float32),
        "load_shape": centred(key_list[1], (3, NZ, NY, NX), 1.0, 6.0, ((1, 64),)),
        "zone_ids": place_ends(jax.random.randint(key_list[2], (NZ, NY, NX), 0, ZONES), jax.random.fold_in(key_list[2], 1), 0, ZONES - 1).astype(jnp.int32),
        "zone_shear": jnp.clip(jnp.exp(jax.random.uniform(key_list[3], (ZONES,), jnp.float32, math.log(0.3), math.log(1.2))), 0.3, 1.2),
        "zone_lame": jnp.clip(jnp.exp(jax.random.uniform(key_list[4], (ZONES,), jnp.float32, math.log(0.3), math.log(1.5))), 0.3, 1.5),
        "amp_table": jnp.clip(jnp.exp(jax.random.uniform(key_list[5], (CYCLES,), jnp.float32, math.log(0.5), math.log(2.0))), 0.5, 2.0),
        "cycle_index": jax.random.permutation(key_list[6], CYCLES).astype(jnp.int32),
    }


DT_FINE = 0.18
DT_COARSE = 0.36
FACE_WEIGHT = 14.0 / 30.0
EDGE_WEIGHT = 3.0 / 30.0
CORNER_WEIGHT = 1.0 / 30.0


def combine(first_vec, second_vec, first_sign, second_sign):
    return tuple(first_sign * first_vec[i] + second_sign * second_vec[i] for i in range(3))


def acceleration(padded, stiff_shear, stiff_bulk, loading):
    layers = padded.shape[1] - 2
    stripes = padded.shape[2] - 2
    columns = padded.shape[3] - 2

    def shifted_by(offset):
        return padded[:, 1 + offset[0]:1 + offset[0] + layers, 1 + offset[1]:1 + offset[1] + stripes, 1 + offset[2]:1 + offset[2] + columns]

    centre = shifted_by((0, 0, 0))
    laplace = jnp.zeros_like(centre)
    for step_z in (-1, 0, 1):
        for step_y in (-1, 0, 1):
            for step_x in (-1, 0, 1):
                reach = abs(step_z) + abs(step_y) + abs(step_x)
                if reach > 0:
                    weight = (FACE_WEIGHT, EDGE_WEIGHT, CORNER_WEIGHT)[reach - 1]
                    laplace = laplace + weight * (shifted_by((step_z, step_y, step_x)) - centre)
    axis_units = ((0, 0, 1), (0, 1, 0), (1, 0, 0))
    coupled = []
    for component in range(3):
        own_unit = axis_units[component]
        along = shifted_by(own_unit)[component] + shifted_by(combine(own_unit, own_unit, -1, 0))[component] - 2.0 * centre[component]
        for other in range(3):
            if other != component:
                other_unit = axis_units[other]
                both_up = shifted_by(combine(own_unit, other_unit, 1, 1))[other]
                up_down = shifted_by(combine(own_unit, other_unit, 1, -1))[other]
                down_up = shifted_by(combine(own_unit, other_unit, -1, 1))[other]
                both_down = shifted_by(combine(own_unit, other_unit, -1, -1))[other]
                along = along + 0.25 * (both_up - up_down - down_up + both_down)
        coupled.append(along)
    coupling = jnp.stack(coupled)
    return stiff_shear * laplace + stiff_bulk * coupling + loading


def propagate(status, step_count, time_step, stiff_shear, stiff_bulk, loading, padder):
    def advance(turn_index, current):
        displaced = current[:3]
        velocity = current[3:]
        velocity = velocity + time_step * acceleration(padder(displaced), stiff_shear, stiff_bulk, loading)
        displaced = displaced + time_step * velocity
        return jnp.concatenate([displaced, velocity], axis=0)

    return lax.fori_loop(0, step_count, advance, status)


def pad_whole(displaced):
    return jnp.pad(displaced, ((0, 0), (1, 1), (1, 1), (1, 1)))


def reference(states, load_shape, zone_ids, zone_shear, zone_lame, amp_table, cycle_index):
    stiff_shear = zone_shear[zone_ids]
    stiff_bulk = zone_lame[zone_ids] + stiff_shear
    load_field = load_shape.astype(jnp.float32)
    results = []
    start_state = states[0]
    for window in range(WINDOWS):
        loading = amp_table[cycle_index[window]] * load_field
        fine_end = propagate(states[window], FINE, DT_FINE, stiff_shear, stiff_bulk, loading, pad_whole)
        coarse_old = propagate(states[window], COARSE, DT_COARSE, stiff_shear, stiff_bulk, loading, pad_whole)
        correction = fine_end - coarse_old
        advanced = propagate(start_state, COARSE, DT_COARSE, stiff_shear, stiff_bulk, loading, pad_whole) + correction
        results.append(advanced)
        start_state = advanced
    return jnp.stack(results)
```

```python
import jax
import jax.numpy as jnp
from jax import lax
from jax.experimental import pallas as pl
from jax.experimental.pallas import tpu as pltpu
from jax.sharding import PartitionSpec as P

FINE = 4
COARSE = 2
DT_FINE = 0.18
DT_COARSE = 0.36
PAD = 8
ROWS = 16
MESH = pl.DeviceIdType.MESH


def kernel(
    windows,
    slabs,
    states,
    load,
    zones,
    shear_table,
    lame_table,
    amp_table,
    cycle_index,
    out,
    disp,
    halo,
    speed,
    drift,
    arrived,
    shear,
    bulk,
    send_sem,
    recv_sem,
    pass_sem,
):
    win = lax.axis_index("win")
    slab = lax.axis_index("slab")
    ny, nx = states.shape[3], states.shape[4]
    inner = pl.ds(PAD, ny)
    has_low = slab > 0
    has_high = slab < slabs - 1
    has_prev = win > 0
    has_next = win < windows - 1

    edge = jnp.zeros((PAD, nx), jnp.float32)
    for c in range(3):
        for slot in range(disp.shape[0]):
            for p in range(2):
                disp[slot, c, p, pl.ds(0, PAD), :] = edge
                disp[slot, c, p, pl.ds(PAD + ny, PAD), :] = edge
        for slot in range(halo.shape[0]):
            for side in range(2):
                halo[slot, side, c, pl.ds(0, PAD), :] = edge
                halo[slot, side, c, pl.ds(PAD + ny, PAD), :] = edge
    plane_zero = jnp.zeros((ny, nx), jnp.float32)
    for side, missing in ((0, slab == 0), (1, slab == slabs - 1)):

        @pl.when(missing)
        def _(side=side):
            for slot in range(halo.shape[0]):
                for c in range(3):
                    halo[slot, side, c, inner, :] = plane_zero

    barrier = pltpu.get_barrier_semaphore()
    for present, target in (
        (has_low, {"slab": slab - 1}),
        (has_high, {"slab": slab + 1}),
        (has_prev, {"win": win - 1}),
        (has_next, {"win": win + 1}),
    ):

        @pl.when(present)
        def _(target=target):
            pl.semaphore_signal(barrier, inc=1, device_id=target, device_id_type=MESH)

    expected = (
        has_low.astype(jnp.int32)
        + has_high.astype(jnp.int32)
        + has_prev.astype(jnp.int32)
        + has_next.astype(jnp.int32)
    )
    pl.semaphore_wait(barrier, expected)

    def halo_copy(source, slot, p):
        return pltpu.make_async_remote_copy(
            src_ref=source,
            dst_ref=halo.at[slot, 1 - p, :, inner, :],
            send_sem=send_sem.at[slot, p],
            recv_sem=recv_sem.at[slot, 1 - p],
            device_id={"slab": slab - 1 + 2 * p},
            device_id_type=MESH,
        )

    def first_source(p):
        return states.at[0, pl.ds(0, 3), p]

    def disp_source(slot, p):
        return disp.at[slot, :, p, inner, :]

    reach = (has_low, has_high)

    def send_plane(source, slot, p):
        @pl.when(reach[p])
        def _():
            halo_copy(source, slot, p).start()

    def await_halo(slot, side):
        @pl.when(reach[side])
        def _():
            halo_copy(disp_source(0, 1 - side), slot, 1 - side).wait_recv()

    for p in range(2):
        send_plane(first_source(p), 0, p)

    for c in range(3):
        for p in range(2):
            disp[0, c, p, inner, :] = states[0, c, p]
            speed[c, p] = states[0, 3 + c, p]
    ids = zones[...]
    mu = jnp.zeros(ids.shape, jnp.float32)
    lame = jnp.zeros(ids.shape, jnp.float32)
    for k in range(shear_table.shape[0]):
        mu = jnp.where(ids == k, shear_table[k], mu)
        lame = jnp.where(ids == k, lame_table[k], lame)
    shear[...] = mu * (1.0 / 30.0)
    bulk[...] = lame + mu
    amp = amp_table[cycle_index[win]]

    lane = lax.broadcasted_iota(jnp.int32, (ROWS, nx), 1)
    first_lane = lane == 0
    last_lane = lane == nx - 1
    tall = ROWS + 2 * PAD

    def left(f):
        return jnp.where(first_lane, 0.0, pltpu.roll(f, 1, 1))

    def right(f):
        return jnp.where(last_lane, 0.0, pltpu.roll(f, nx - 1, 1))

    def above(f):
        return pltpu.roll(f, 1, 0)[PAD : PAD + ROWS]

    def below(f):
        return pltpu.roll(f, tall - 1, 0)[PAD : PAD + ROWS]

    def core(f):
        return f[PAD : PAD + ROWS]

    def plane_step(slot, hslot, p, h, velocity, loaded, finish):
        def body(block, carry):
            start = pl.multiple_of(block * ROWS, ROWS)
            rows = pl.ds(start, ROWS)
            window = pl.ds(start, tall)
            low, mid, high = [], [], []
            for c in range(3):
                own = [disp[slot, c, q, window, :] for q in range(2)]
                mid.append(own[p])
                low.append(halo[hslot, 0, c, window, :] if p == 0 else own[0])
                high.append(own[1] if p == 0 else halo[hslot, 1, c, window, :])
            zs = [low[c] + high[c] for c in range(3)]
            zd = [high[c] - low[c] for c in range(3)]
            laps = []
            for c in range(3):
                face = 3.0 * zs[c] + 14.0 * mid[c]
                diag = zs[c] + 3.0 * mid[c]
                side = core(face) + above(diag) + below(diag)
                laps.append(
                    14.0 * core(zs[c])
                    - 128.0 * core(mid[c])
                    + (above(face) + below(face))
                    + (left(side) + right(side))
                )
            ux, uy = mid[0], mid[1]
            uy_up, uy_down = below(uy), above(uy)
            cross = (uy_up - uy_down) + core(zd[2])
            ux_core = core(ux)
            ux_left, ux_right = left(ux_core), right(ux_core)
            lead_x = (ux_left + ux_right - 2.0 * ux_core) + 0.25 * (right(cross) - left(cross))
            row_diff = below(ux) - above(ux)
            lead_y = (uy_up + uy_down - 2.0 * core(uy)) + 0.25 * (
                (right(row_diff) - left(row_diff)) + (below(zd[2]) - above(zd[2]))
            )
            zx = core(zd[0])
            lead_z = (core(zs[2]) - 2.0 * core(mid[2])) + 0.25 * (
                (right(zx) - left(zx)) + (below(zd[1]) - above(zd[1]))
            )
            mu_rows = shear[p, rows, :]
            bulk_rows = bulk[p, rows, :]
            for c, lead in enumerate((lead_x, lead_y, lead_z)):
                rate = mu_rows * laps[c] + bulk_rows * lead
                if loaded:
                    rate = rate + amp * load[c, p, rows, :].astype(jnp.float32)
                moved = velocity[c, p, rows, :] + h * rate
                finish(c, p, start, moved, core(mid[c]) + h * moved)
            return carry

        lax.fori_loop(0, ny // ROWS, body, 0)

    def keep(slot, velocity):
        def finish(c, p, start, moved, placed):
            velocity[c, p, pl.ds(start, ROWS), :] = moved
            disp[slot, c, p, pl.ds(start + PAD, ROWS), :] = placed

        return finish

    for step in range(FINE):
        for p in range(2):
            await_halo(step, p)
            plane_step(step, step, p, DT_FINE, speed, True, keep(step + 1, speed))
            if step + 1 < FINE:
                send_plane(disp_source(step + 1, p), step + 1, p)

    pass_on = pltpu.make_async_remote_copy(
        src_ref=out.at[0],
        dst_ref=arrived,
        send_sem=pass_sem.at[0],
        recv_sem=pass_sem.at[1],
        device_id={"win": win + 1},
        device_id_type=MESH,
    )

    @pl.when(win == 0)
    def _():
        for c in range(3):
            for p in range(2):
                out[0, c, p] = disp[FINE, c, p, inner, :]
                out[0, 3 + c, p] = speed[c, p]

    @pl.when(has_prev)
    def _():
        pass_on.wait_recv()
        base = FINE + 1
        for p in range(2):
            for c in range(3):
                disp[base, c, p, inner, :] = arrived[c, p] - states[0, c, p]
            send_plane(disp_source(base, p), FINE, p)
        for p in range(2):
            for c in range(3):
                drift[c, p] = arrived[3 + c, p] - states[0, 3 + c, p]

        def conclude(c, p, start, moved, placed):
            rows = pl.ds(start, ROWS)
            out[0, c, p, rows, :] = disp[FINE, c, p, pl.ds(start + PAD, ROWS), :] + placed
            out[0, 3 + c, p, rows, :] = speed[c, p, rows, :] + moved

        for step in range(COARSE):
            for p in range(2):
                await_halo(FINE + step, p)
                last = step + 1 == COARSE
                finish = conclude if last else keep(base + step + 1, drift)
                plane_step(base + step, FINE + step, p, DT_COARSE, drift, False, finish)
                if not last:
                    send_plane(disp_source(base + step + 1, p), FINE + step + 1, p)

    @pl.when(has_next)
    def _():
        pass_on.start()

    for slot in range(FINE):
        for p in range(2):

            @pl.when(reach[p])
            def _(slot=slot, p=p):
                halo_copy(disp_source(slot, p), slot, p).wait_send()

    for slot in range(FINE, FINE + COARSE):
        for p in range(2):

            @pl.when(jnp.logical_and(reach[p], has_prev))
            def _(slot=slot, p=p):
                halo_copy(disp_source(slot, p), slot, p).wait_send()

    @pl.when(has_next)
    def _():
        pass_on.wait_send()


def solution(mesh):
    windows, slabs = mesh.shape["win"], mesh.shape["slab"]

    def shards(states, load, zones, shear_table, lame_table, amp_table, cycle_index):
        _, _, nz, ny, nx = states.shape
        vmem = pl.BlockSpec(memory_space=pltpu.VMEM)
        smem = pl.BlockSpec(memory_space=pltpu.SMEM)
        f32 = jnp.float32
        steps = FINE + COARSE
        tall = ny + 2 * PAD
        return pl.pallas_call(
            lambda *refs: kernel(windows, slabs, *refs),
            out_shape=jax.ShapeDtypeStruct(states.shape, f32),
            in_specs=[vmem] * 3 + [smem] * 4,
            out_specs=vmem,
            scratch_shapes=[
                pltpu.VMEM((steps + 1, 3, nz, tall, nx), f32),
                pltpu.VMEM((steps, 2, 3, tall, nx), f32),
                pltpu.VMEM((3, nz, ny, nx), f32),
                pltpu.VMEM((3, nz, ny, nx), f32),
                pltpu.VMEM((6, nz, ny, nx), f32),
                pltpu.VMEM((nz, ny, nx), f32),
                pltpu.VMEM((nz, ny, nx), f32),
                pltpu.SemaphoreType.DMA((steps, 2)),
                pltpu.SemaphoreType.DMA((steps, 2)),
                pltpu.SemaphoreType.DMA((2,)),
            ],
            compiler_params=pltpu.CompilerParams(
                collective_id=0, has_side_effects=True, vmem_limit_bytes=48 * 2**20
            ),
            name="parareal",
        )(states, load, zones, shear_table, lame_table, amp_table, cycle_index)

    placed = (
        P("win", None, "slab", None, None),
        P(None, "slab", None, None),
        P("slab", None, None),
        P(),
        P(),
        P(),
        P(),
    )
    return jax.shard_map(
        shards,
        mesh=mesh,
        in_specs=placed,
        out_specs=P("win", None, "slab", None, None),
        check_vma=False,
    )
```

```python
import jax
import jax.numpy as jnp
from jax import lax
from jax.experimental import pallas as pl
from jax.experimental.pallas import tpu as pltpu
from jax.sharding import PartitionSpec as P

FINE = 4
DT_FINE = 0.18
DT_COARSE = 0.36
PAD = 8
ROWS = 16
MESH = pl.DeviceIdType.MESH


def stencil(low, mid, high, trim):
    tall, nx = mid[0].shape
    size = tall - 2 * trim
    lane = lax.broadcasted_iota(jnp.int32, (size, nx), 1)
    first_lane = lane == 0
    last_lane = lane == nx - 1

    def left(f):
        return jnp.where(first_lane, 0.0, pltpu.roll(f, 1, 1))

    def right(f):
        return jnp.where(last_lane, 0.0, pltpu.roll(f, nx - 1, 1))

    def core(f):
        return f[trim : trim + size]

    def above(f):
        return core(pltpu.roll(f, 1, 0))

    def below(f):
        return core(pltpu.roll(f, tall - 1, 0))

    zs = [low[c] + high[c] for c in range(3)]
    zd = [high[c] - low[c] for c in range(3)]
    laps = []
    for c in range(3):
        face = 3.0 * zs[c] + 14.0 * mid[c]
        diag = zs[c] + 3.0 * mid[c]
        side = core(face) + above(diag) + below(diag)
        laps.append(
            14.0 * core(zs[c])
            - 128.0 * core(mid[c])
            + (above(face) + below(face))
            + (left(side) + right(side))
        )
    ux, uy = mid[0], mid[1]
    uy_up, uy_down = below(uy), above(uy)
    cross = (uy_up - uy_down) + core(zd[2])
    ux_core = core(ux)
    lead_x = (left(ux_core) + right(ux_core) - 2.0 * ux_core) + 0.25 * (right(cross) - left(cross))
    row_diff = below(ux) - above(ux)
    lead_y = (uy_up + uy_down - 2.0 * core(uy)) + 0.25 * (
        (right(row_diff) - left(row_diff)) + (below(zd[2]) - above(zd[2]))
    )
    zx = core(zd[0])
    lead_z = (core(zs[2]) - 2.0 * core(mid[2])) + 0.25 * (
        (right(zx) - left(zx)) + (below(zd[1]) - above(zd[1]))
    )
    return laps, (lead_x, lead_y, lead_z)


def kernel(
    windows,
    slabs,
    states_hbm,
    load_hbm,
    zones_hbm,
    shear_hbm,
    lame_hbm,
    amp_hbm,
    cycle_hbm,
    out,
    states,
    load,
    zones,
    shear_table,
    lame_table,
    amp_table,
    cycle_index,
    disp,
    halo,
    speed,
    fine_end,
    next_zones,
    shear,
    bulk,
    starts,
    fines,
    ends,
    wide_disp,
    wide_speed,
    mid_disp,
    mid_speed,
    rim_out,
    rim_in,
    load_sem,
    zone_send,
    zone_recv,
    halo_send,
    halo_recv,
    start_send,
    start_recv,
    fine_send,
    fine_recv,
    home_send,
    home_recv,
    wide_send,
    wide_recv,
):
    win = lax.axis_index("win")
    slab = lax.axis_index("slab")
    ny, nx = states.shape[2], states.shape[3]
    part = ny // windows
    wide = part + 2 * PAD
    inner = pl.ds(PAD, ny)
    own_rows = pl.ds(pl.multiple_of(win * part, 8), part)
    has_slab = (slab > 0, slab < slabs - 1)
    has_win = (win > 0, win < windows - 1)

    pairs = (
        (states_hbm.at[0], states),
        (zones_hbm, zones),
        (load_hbm, load),
        (shear_hbm, shear_table),
        (lame_hbm, lame_table),
        (amp_hbm, amp_table),
        (cycle_hbm, cycle_index),
    )
    loads = [pltpu.make_async_copy(a, b, load_sem.at[k]) for k, (a, b) in enumerate(pairs)]
    for copy in loads:
        copy.start()

    around = [(a, b) for a in (-1, 0, 1) for b in (-1, 0, 1) if (a, b) != (0, 0)]

    def present(step):
        a, b = step
        found = None
        if a:
            found = has_slab[(a + 1) // 2]
        if b:
            side = has_win[(b + 1) // 2]
            found = side if found is None else jnp.logical_and(found, side)
        return found

    barrier = pltpu.get_barrier_semaphore()
    expected = jnp.int32(windows - 1)
    for k in range(1, windows):
        target = {"win": lax.rem(win + k, windows)}
        pl.semaphore_signal(barrier, inc=1, device_id=target, device_id_type=MESH)
    for a, b in around:
        if a:
            there = present((a, b))
            expected = expected + there.astype(jnp.int32)

            @pl.when(there)
            def _(a=a, b=b):
                target = {"win": win + b, "slab": slab + a}
                pl.semaphore_signal(barrier, inc=1, device_id=target, device_id_type=MESH)

    edge = jnp.zeros((PAD, nx), jnp.float32)
    for c in range(3):
        for slot in range(disp.shape[0]):
            for p in range(2):
                disp[slot, c, p, pl.ds(0, PAD), :] = edge
                disp[slot, c, p, pl.ds(PAD + ny, PAD), :] = edge
        for slot in range(halo.shape[0]):
            for side in range(2):
                halo[slot, side, c, pl.ds(0, PAD), :] = edge
                halo[slot, side, c, pl.ds(PAD + ny, PAD), :] = edge
    plane_zero = jnp.zeros((ny, nx), jnp.float32)
    for side in range(2):

        @pl.when(jnp.logical_not(has_slab[side]))
        def _(side=side):
            for slot in range(halo.shape[0]):
                for c in range(3):
                    halo[slot, side, c, inner, :] = plane_zero

    def clear(n, carry):
        for c in range(3):
            wide_disp[n, c] = jnp.zeros(wide_disp.shape[2:], jnp.float32)
            wide_speed[n, c] = jnp.zeros(wide_speed.shape[2:], jnp.float32)
        return carry

    lax.fori_loop(0, wide_disp.shape[0], clear, 0)
    tall_zero = jnp.zeros(shear.shape[1:], jnp.float32)
    for q in range(4):
        shear[q] = tall_zero
        bulk[q] = tall_zero

    pl.semaphore_wait(barrier, expected)

    def halo_copy(source, slot, p):
        return pltpu.make_async_remote_copy(
            src_ref=source,
            dst_ref=halo.at[slot, 1 - p, :, inner, :],
            send_sem=halo_send.at[slot, p],
            recv_sem=halo_recv.at[slot, 1 - p],
            device_id={"slab": slab - 1 + 2 * p},
            device_id_type=MESH,
        )

    def disp_source(slot, p):
        return disp.at[slot, :, p, inner, :]

    def send_plane(source, slot, p):
        @pl.when(has_slab[p])
        def _():
            halo_copy(source, slot, p).start()

    def await_halo(slot, side):
        @pl.when(has_slab[side])
        def _():
            halo_copy(disp_source(0, 1 - side), slot, 1 - side).wait_recv()

    def zone_copy(p):
        return pltpu.make_async_remote_copy(
            src_ref=zones.at[p],
            dst_ref=next_zones.at[1 - p],
            send_sem=zone_send.at[p],
            recv_sem=zone_recv.at[1 - p],
            device_id={"slab": slab - 1 + 2 * p},
            device_id_type=MESH,
        )

    def share(source, target, send, recv, k):
        other = lax.rem(win + k, windows)
        return pltpu.make_async_remote_copy(
            src_ref=source.at[:, :, pl.ds(pl.multiple_of(other * part, 8), part), :],
            dst_ref=target.at[win],
            send_sem=send.at[k],
            recv_sem=recv.at[win],
            device_id={"win": other},
            device_id_type=MESH,
        )

    def shared(target, recv, n):
        return pltpu.make_async_remote_copy(
            src_ref=target.at[n],
            dst_ref=target.at[n],
            send_sem=recv.at[n],
            recv_sem=recv.at[n],
            device_id={"win": lax.rem(win + 1, windows)},
            device_id_type=MESH,
        )

    loads[0].wait()
    for p in range(2):
        send_plane(states.at[pl.ds(0, 3), p], 0, p)
    loads[1].wait()
    for p in range(2):

        @pl.when(has_slab[p])
        def _(p=p):
            zone_copy(p).start()

    for k in range(1, windows):
        share(states, starts, start_send, start_recv, k).start()

    for c in range(3):
        for p in range(2):
            disp[0, c, p, inner, :] = states[c, p]
            speed[c, p] = states[3 + c, p]
    for copy in loads[2:]:
        copy.wait()

    def material(ids, q):
        mu = jnp.zeros(ids.shape, jnp.float32)
        lame = jnp.zeros(ids.shape, jnp.float32)
        for k in range(shear_table.shape[0]):
            mu = jnp.where(ids == k, shear_table[k], mu)
            lame = jnp.where(ids == k, lame_table[k], lame)
        shear[q, inner, :] = mu * (1.0 / 30.0)
        bulk[q, inner, :] = lame + mu

    for p in range(2):
        material(zones[p], 1 + p)
    amp = amp_table[cycle_index[win]]

    for step in range(FINE):
        for p in range(2):
            await_halo(step, p)

            def body(block, carry, step=step, p=p):
                start = pl.multiple_of(block * ROWS, ROWS)
                rows = pl.ds(start, ROWS)
                shifted = pl.ds(start + PAD, ROWS)
                window = pl.ds(start, ROWS + 2 * PAD)
                low, mid, high = [], [], []
                for c in range(3):
                    own = [disp[step, c, q, window, :] for q in range(2)]
                    mid.append(own[p])
                    low.append(halo[step, 0, c, window, :] if p == 0 else own[0])
                    high.append(own[1] if p == 0 else halo[step, 1, c, window, :])
                laps, leads = stencil(low, mid, high, PAD)
                mu = shear[1 + p, shifted, :]
                stiff = bulk[1 + p, shifted, :]
                for c in range(3):
                    rate = mu * laps[c] + stiff * leads[c]
                    rate = rate + amp * load[c, p, rows, :].astype(jnp.float32)
                    moved = speed[c, p, rows, :] + DT_FINE * rate
                    placed = mid[c][PAD : PAD + ROWS] + DT_FINE * moved
                    if step + 1 < FINE:
                        speed[c, p, rows, :] = moved
                        disp[step + 1, c, p, shifted, :] = placed
                    else:
                        fine_end[c, p, rows, :] = placed
                        fine_end[3 + c, p, rows, :] = moved
                return carry

            lax.fori_loop(0, ny // ROWS, body, 0)
            if step + 1 < FINE:
                send_plane(disp_source(step + 1, p), step + 1, p)

    for k in range(1, windows):
        share(fine_end, fines, fine_send, fine_recv, k).start()
    fines[win] = fine_end[:, :, own_rows, :]
    starts[win] = states[:, :, own_rows, :]

    @pl.when(win == 0)
    def _():
        out[0] = fine_end[...]

    for side in range(2):

        @pl.when(has_slab[side])
        def _(side=side):
            zone_copy(1 - side).wait_recv()
            material(next_zones[side], 3 * side)

    centre = pl.ds(PAD, part)
    deep = 2

    def wide_copies(n, step):
        a, b = step
        which = around.index(step)
        if b == 0:
            sources = (wide_disp.at[n, :, pl.ds(2, 2), centre, :],)
            sources += (wide_speed.at[n, :, pl.ds(1 + (a + 1) // 2, 1), centre, :],)
            targets = (wide_disp.at[n, :, pl.ds(2 - 2 * a, 2), centre, :],)
            targets += (wide_speed.at[n, :, pl.ds(0 if a > 0 else 3, 1), centre, :],)
        else:
            planes = pl.ds(0, 2) if a == 0 else pl.ds((a + 1) // 2, 1)
            mirror = around.index((-a, -b))
            edge_rows = rim_out.at[n, (b + 1) // 2]
            landing = rim_in.at[n, mirror]
            sources = (edge_rows.at[pl.ds(0, 3)], edge_rows.at[pl.ds(3, 3), planes])
            targets = (landing.at[pl.ds(0, 3)], landing.at[pl.ds(3, 3), planes])
        came = around.index((-a, -b))
        return [
            pltpu.make_async_remote_copy(
                src_ref=source,
                dst_ref=target,
                send_sem=wide_send.at[n, which, k],
                recv_sem=wide_recv.at[n, came, k],
                device_id={"win": win + b, "slab": slab + a},
                device_id_type=MESH,
            )
            for k, (source, target) in enumerate(zip(sources, targets))
        ]

    def turn(n, carry):
        @pl.when(jnp.logical_and(n == 1, win != 0))
        def _():
            shared(fines, fine_recv, 0).wait_recv()

        @pl.when(n != win)
        def _():
            shared(starts, start_recv, n).wait_recv()

        previous = ends.at[n - 1]

        @pl.when(n == 1)
        def _():
            ends[0] = fines[0]

        for c in range(3):
            for p in range(2):
                gap = previous[c, p] - starts[n, c, p]
                gap_speed = previous[3 + c, p] - starts[n, 3 + c, p]
                wide_disp[n, c, 2 + p, centre, :] = gap
                wide_speed[n, c, 1 + p, centre, :] = gap_speed
                for side in range(2):
                    first = (part - deep) * side
                    rim_out[n, side, c, p] = gap[first : first + deep]
                    rim_out[n, side, 3 + c, p] = gap_speed[first : first + deep]
        for step in around:

            @pl.when(present(step))
            def _(step=step):
                for copy in wide_copies(n, step):
                    copy.start()

        for step in around:

            @pl.when(present(step))
            def _(step=step):
                a, b = step
                for copy in wide_copies(n, (-a, -b)):
                    copy.wait_recv()
                if b:
                    which = around.index(step)
                    rows = pl.ds(PAD - deep if b < 0 else PAD + part, deep)
                    for c in range(3):
                        for p in range(2):
                            wide_disp[n, c, 2 + 2 * a + p, rows, :] = rim_in[n, which, c, p]
                        for p in range(2) if a == 0 else ((1 if a < 0 else 0),):
                            q = 1 + 2 * a + p
                            wide_speed[n, c, q, rows, :] = rim_in[n, which, 3 + c, p]

        rows = pl.ds(pl.multiple_of(win * part, 8), wide)
        for q in range(4):
            planes = [[wide_disp[n, c, q + k] for c in range(3)] for k in range(3)]
            laps, leads = stencil(*planes, 0)
            mu = shear[q, rows, :]
            stiff = bulk[q, rows, :]
            for c in range(3):
                rate = mu * laps[c] + stiff * leads[c]
                moved = wide_speed[n, c, q] + DT_COARSE * rate
                mid_disp[c, q] = planes[1][c] + DT_COARSE * moved
                if q in (1, 2):
                    mid_speed[c, q - 1] = moved[PAD : PAD + part]

        @pl.when(n != win)
        def _():
            shared(fines, fine_recv, n).wait_recv()

        rows = pl.ds(pl.multiple_of(win * part + PAD, 8), part)
        for p in range(2):
            planes = [[mid_disp[c, p + k] for c in range(3)] for k in range(3)]
            laps, leads = stencil(*planes, PAD)
            mu = shear[1 + p, rows, :]
            stiff = bulk[1 + p, rows, :]
            for c in range(3):
                rate = mu * laps[c] + stiff * leads[c]
                moved = mid_speed[c, p] + DT_COARSE * rate
                placed = planes[1][c][PAD : PAD + part] + DT_COARSE * moved
                ends[n, c, p] = fines[n, c, p] + placed
                ends[n, 3 + c, p] = fines[n, 3 + c, p] + moved

        @pl.when(n == win)
        def _():
            out[0, :, :, own_rows, :] = ends[n]

        @pl.when(n != win)
        def _():
            home(n).start()

        for step in around:

            @pl.when(present(step))
            def _(step=step):
                for copy in wide_copies(n, step):
                    copy.wait_send()

        return carry

    def home(n):
        return pltpu.make_async_remote_copy(
            src_ref=ends.at[n],
            dst_ref=out.at[0, :, :, own_rows, :],
            send_sem=home_send.at[n],
            recv_sem=home_recv.at[win],
            device_id={"win": n},
            device_id_type=MESH,
        )

    lax.fori_loop(1, windows, turn, 0)

    for n in range(windows):

        @pl.when(n != win)
        def _(n=n):
            if n == 0:
                shared(starts, start_recv, 0).wait_recv()
            else:
                home(n).wait_send()

        @pl.when(jnp.logical_and(win != 0, n != win))
        def _(n=n):
            rows = pl.ds(n * part, part)
            pltpu.make_async_remote_copy(
                src_ref=ends.at[0],
                dst_ref=out.at[0, :, :, rows, :],
                send_sem=home_send.at[0],
                recv_sem=home_recv.at[n],
                device_id={"win": lax.rem(win + 1, windows)},
                device_id_type=MESH,
            ).wait_recv()

    for k in range(1, windows):
        share(states, starts, start_send, start_recv, k).wait_send()
        share(fine_end, fines, fine_send, fine_recv, k).wait_send()
    for p in range(2):

        @pl.when(has_slab[p])
        def _(p=p):
            zone_copy(p).wait_send()
            for slot in range(FINE):
                halo_copy(disp_source(slot, p), slot, p).wait_send()


def solution(mesh):
    windows, slabs = mesh.shape["win"], mesh.shape["slab"]

    def shards(states, load, zones, shear_table, lame_table, amp_table, cycle_index):
        _, _, nz, ny, nx = states.shape
        f32 = jnp.float32
        tall = ny + 2 * PAD
        part = ny // windows
        wide = part + 2 * PAD
        dma = pltpu.SemaphoreType.DMA
        return pl.pallas_call(
            lambda *refs: kernel(windows, slabs, *refs),
            out_shape=jax.ShapeDtypeStruct(states.shape, f32),
            in_specs=[pl.BlockSpec(memory_space=pl.ANY)] * 7,
            out_specs=pl.BlockSpec(memory_space=pltpu.VMEM),
            scratch_shapes=[
                pltpu.VMEM(states.shape[1:], f32),
                pltpu.VMEM(load.shape, load.dtype),
                pltpu.VMEM(zones.shape, jnp.int32),
                pltpu.SMEM(shear_table.shape, f32),
                pltpu.SMEM(lame_table.shape, f32),
                pltpu.SMEM(amp_table.shape, f32),
                pltpu.SMEM(cycle_index.shape, jnp.int32),
                pltpu.VMEM((FINE, 3, nz, tall, nx), f32),
                pltpu.VMEM((FINE, 2, 3, tall, nx), f32),
                pltpu.VMEM((3, nz, ny, nx), f32),
                pltpu.VMEM((6, nz, ny, nx), f32),
                pltpu.VMEM((2, ny, nx), jnp.int32),
                pltpu.VMEM((4, tall, nx), f32),
                pltpu.VMEM((4, tall, nx), f32),
                pltpu.VMEM((windows, 6, nz, part, nx), f32),
                pltpu.VMEM((windows, 6, nz, part, nx), f32),
                pltpu.VMEM((windows, 6, nz, part, nx), f32),
                pltpu.VMEM((windows, 3, 6, wide, nx), f32),
                pltpu.VMEM((windows, 3, 4, wide, nx), f32),
                pltpu.VMEM((3, 4, wide, nx), f32),
                pltpu.VMEM((3, 2, part, nx), f32),
                pltpu.VMEM((windows, 2, 6, 2, 2, nx), f32),
                pltpu.VMEM((windows, 8, 6, 2, 2, nx), f32),
                dma((7,)),
                dma((2,)),
                dma((2,)),
                dma((FINE, 2)),
                dma((FINE, 2)),
                dma((windows,)),
                dma((windows,)),
                dma((windows,)),
                dma((windows,)),
                dma((windows,)),
                dma((windows,)),
                dma((windows, 8, 2)),
                dma((windows, 8, 2)),
            ],
            compiler_params=pltpu.CompilerParams(
                collective_id=0, has_side_effects=True, vmem_limit_bytes=60 * 2**20
            ),
            name="parareal",
        )(states, load, zones, shear_table, lame_table, amp_table, cycle_index)

    placed = (
        P("win", None, "slab", None, None),
        P(None, "slab", None, None),
        P("slab", None, None),
        P(),
        P(),
        P(),
        P(),
    )
    return jax.shard_map(
        shards,
        mesh=mesh,
        in_specs=placed,
        out_specs=P("win", None, "slab", None, None),
        check_vma=False,
    )
```

```python
import jax
import jax.numpy as jnp
from jax import lax
from jax.experimental import pallas as pl
from jax.experimental.pallas import tpu as pltpu
from jax.sharding import PartitionSpec as P

FINE = 4
DT_FINE = 0.18
DT_COARSE = 0.36
PAD = 8
ROWS = 16
MESH = pl.DeviceIdType.MESH


def stencil(low, mid, high, trim):
    tall, nx = mid[0].shape
    size = tall - 2 * trim
    lane = lax.broadcasted_iota(jnp.int32, (size, nx), 1)
    first_lane = lane == 0
    last_lane = lane == nx - 1

    def left(f):
        return jnp.where(first_lane, 0.0, pltpu.roll(f, 1, 1))

    def right(f):
        return jnp.where(last_lane, 0.0, pltpu.roll(f, nx - 1, 1))

    def core(f):
        return f[trim : trim + size]

    def above(f):
        return core(pltpu.roll(f, 1, 0))

    def below(f):
        return core(pltpu.roll(f, tall - 1, 0))

    zs = [low[c] + high[c] for c in range(3)]
    zd = [high[c] - low[c] for c in range(3)]
    laps = []
    for c in range(3):
        face = 3.0 * zs[c] + 14.0 * mid[c]
        diag = zs[c] + 3.0 * mid[c]
        side = core(face) + above(diag) + below(diag)
        laps.append(
            14.0 * core(zs[c])
            - 128.0 * core(mid[c])
            + (above(face) + below(face))
            + (left(side) + right(side))
        )
    ux, uy = mid[0], mid[1]
    uy_up, uy_down = below(uy), above(uy)
    cross = (uy_up - uy_down) + core(zd[2])
    ux_core = core(ux)
    lead_x = (left(ux_core) + right(ux_core) - 2.0 * ux_core) + 0.25 * (right(cross) - left(cross))
    row_diff = below(ux) - above(ux)
    lead_y = (uy_up + uy_down - 2.0 * core(uy)) + 0.25 * (
        (right(row_diff) - left(row_diff)) + (below(zd[2]) - above(zd[2]))
    )
    zx = core(zd[0])
    lead_z = (core(zs[2]) - 2.0 * core(mid[2])) + 0.25 * (
        (right(zx) - left(zx)) + (below(zd[1]) - above(zd[1]))
    )
    return laps, (lead_x, lead_y, lead_z)


def kernel(
    windows,
    slabs,
    states_hbm,
    load_hbm,
    zones_hbm,
    shear_hbm,
    lame_hbm,
    amp_hbm,
    cycle_hbm,
    out,
    states,
    load,
    zones,
    shear_table,
    lame_table,
    amp_table,
    cycle_index,
    disp,
    halo,
    speed,
    fine_end,
    next_zones,
    shear,
    bulk,
    starts,
    fines,
    ends,
    wide_disp,
    wide_speed,
    mid_disp,
    mid_speed,
    rim_out,
    rim_in,
    load_sem,
    zone_send,
    zone_recv,
    halo_send,
    halo_recv,
    start_send,
    start_recv,
    fine_send,
    fine_recv,
    home_send,
    home_recv,
    wide_send,
    wide_recv,
):
    win = lax.axis_index("win")
    slab = lax.axis_index("slab")
    ny, nx = states.shape[2], states.shape[3]
    part = ny // windows
    wide = part + 2 * PAD
    inner = pl.ds(PAD, ny)
    own_rows = pl.ds(pl.multiple_of(win * part, 8), part)
    has_slab = (slab > 0, slab < slabs - 1)
    has_win = (win > 0, win < windows - 1)

    pairs = (
        (states_hbm.at[0], states),
        (zones_hbm, zones),
        (load_hbm, load),
        (shear_hbm, shear_table),
        (lame_hbm, lame_table),
        (amp_hbm, amp_table),
        (cycle_hbm, cycle_index),
    )
    loads = [pltpu.make_async_copy(a, b, load_sem.at[k]) for k, (a, b) in enumerate(pairs)]
    for copy in loads:
        copy.start()

    around = [(a, b) for a in (-1, 0, 1) for b in (-1, 0, 1) if (a, b) != (0, 0)]

    def present(step):
        a, b = step
        found = None
        if a:
            found = has_slab[(a + 1) // 2]
        if b:
            side = has_win[(b + 1) // 2]
            found = side if found is None else jnp.logical_and(found, side)
        return found

    barrier = pltpu.get_barrier_semaphore()
    expected = jnp.int32(windows - 1)
    for k in range(1, windows):
        target = {"win": lax.rem(win + k, windows)}
        pl.semaphore_signal(barrier, inc=1, device_id=target, device_id_type=MESH)
    for a, b in around:
        if a:
            there = present((a, b))
            expected = expected + there.astype(jnp.int32)

            @pl.when(there)
            def _(a=a, b=b):
                target = {"win": win + b, "slab": slab + a}
                pl.semaphore_signal(barrier, inc=1, device_id=target, device_id_type=MESH)

    edge = jnp.zeros((PAD, nx), jnp.float32)
    for c in range(3):
        for slot in range(disp.shape[0]):
            for p in range(2):
                disp[slot, c, p, pl.ds(0, PAD), :] = edge
                disp[slot, c, p, pl.ds(PAD + ny, PAD), :] = edge
        for slot in range(halo.shape[0]):
            for side in range(2):
                halo[slot, side, c, pl.ds(0, PAD), :] = edge
                halo[slot, side, c, pl.ds(PAD + ny, PAD), :] = edge
    plane_zero = jnp.zeros((ny, nx), jnp.float32)
    for side in range(2):

        @pl.when(jnp.logical_not(has_slab[side]))
        def _(side=side):
            for slot in range(halo.shape[0]):
                for c in range(3):
                    halo[slot, side, c, inner, :] = plane_zero

    def clear(n, carry):
        for c in range(3):
            wide_disp[n, c] = jnp.zeros(wide_disp.shape[2:], jnp.float32)
            wide_speed[n, c] = jnp.zeros(wide_speed.shape[2:], jnp.float32)
        return carry

    lax.fori_loop(0, wide_disp.shape[0], clear, 0)
    tall_zero = jnp.zeros(shear.shape[1:], jnp.float32)
    for q in range(4):
        shear[q] = tall_zero
        bulk[q] = tall_zero

    pl.semaphore_wait(barrier, expected)

    blocks = ny // ROWS

    def halo_copy(slot, p, block):
        start = pl.multiple_of(block * ROWS, ROWS)
        shifted = pl.ds(start + PAD, ROWS)
        if slot == 0:
            source = states.at[pl.ds(0, 3), p, pl.ds(start, ROWS), :]
        else:
            source = disp.at[slot, :, p, shifted, :]
        return pltpu.make_async_remote_copy(
            src_ref=source,
            dst_ref=halo.at[slot, 1 - p, :, shifted, :],
            send_sem=halo_send.at[slot, p, block],
            recv_sem=halo_recv.at[slot, 1 - p, block],
            device_id={"slab": slab - 1 + 2 * p},
            device_id_type=MESH,
        )

    def send_chunk(slot, p, block):
        @pl.when(has_slab[p])
        def _():
            halo_copy(slot, p, block).start()

    def await_chunk(slot, block):
        for side in range(2):

            @pl.when(has_slab[side])
            def _(side=side):
                halo_copy(slot, 1 - side, block).wait_recv()

    def zone_copy(p):
        return pltpu.make_async_remote_copy(
            src_ref=zones.at[p],
            dst_ref=next_zones.at[1 - p],
            send_sem=zone_send.at[p],
            recv_sem=zone_recv.at[1 - p],
            device_id={"slab": slab - 1 + 2 * p},
            device_id_type=MESH,
        )

    def share(source, target, send, recv, k):
        other = lax.rem(win + k, windows)
        return pltpu.make_async_remote_copy(
            src_ref=source.at[:, :, pl.ds(pl.multiple_of(other * part, 8), part), :],
            dst_ref=target.at[win],
            send_sem=send.at[k],
            recv_sem=recv.at[win],
            device_id={"win": other},
            device_id_type=MESH,
        )

    def shared(target, recv, n):
        return pltpu.make_async_remote_copy(
            src_ref=target.at[n],
            dst_ref=target.at[n],
            send_sem=recv.at[n],
            recv_sem=recv.at[n],
            device_id={"win": lax.rem(win + 1, windows)},
            device_id_type=MESH,
        )

    loads[0].wait()
    for block in range(blocks):
        for p in range(2):
            send_chunk(0, p, block)
    loads[1].wait()
    for p in range(2):

        @pl.when(has_slab[p])
        def _(p=p):
            zone_copy(p).start()

    for c in range(3):
        for p in range(2):
            disp[0, c, p, inner, :] = states[c, p]
            speed[c, p] = states[3 + c, p]
    for copy in loads[2:]:
        copy.wait()

    def material(ids, q):
        mu = jnp.zeros(ids.shape, jnp.float32)
        lame = jnp.zeros(ids.shape, jnp.float32)
        for k in range(shear_table.shape[0]):
            mu = jnp.where(ids == k, shear_table[k], mu)
            lame = jnp.where(ids == k, lame_table[k], lame)
        shear[q, inner, :] = mu * (1.0 / 30.0)
        bulk[q, inner, :] = lame + mu

    for p in range(2):
        material(zones[p], 1 + p)
    amp = amp_table[cycle_index[win]]

    for step in range(FINE):

        @pl.when((win + 1) // 2 == step + 1)
        def _():
            for k in range(1, windows):
                share(states, starts, start_send, start_recv, k).start()

        await_chunk(step, 0)

        def body(block, carry, step=step):
            @pl.when(block + 1 < blocks)
            def _():
                await_chunk(step, block + 1)

            start = pl.multiple_of(block * ROWS, ROWS)
            rows = pl.ds(start, ROWS)
            shifted = pl.ds(start + PAD, ROWS)
            window = pl.ds(start, ROWS + 2 * PAD)
            for p in range(2):
                low, mid, high = [], [], []
                for c in range(3):
                    own = [disp[step, c, q, window, :] for q in range(2)]
                    mid.append(own[p])
                    low.append(halo[step, 0, c, window, :] if p == 0 else own[0])
                    high.append(own[1] if p == 0 else halo[step, 1, c, window, :])
                laps, leads = stencil(low, mid, high, PAD)
                mu = shear[1 + p, shifted, :]
                stiff = bulk[1 + p, shifted, :]
                for c in range(3):
                    rate = mu * laps[c] + stiff * leads[c]
                    rate = rate + amp * load[c, p, rows, :].astype(jnp.float32)
                    moved = speed[c, p, rows, :] + DT_FINE * rate
                    placed = mid[c][PAD : PAD + ROWS] + DT_FINE * moved
                    if step + 1 < FINE:
                        speed[c, p, rows, :] = moved
                        disp[step + 1, c, p, shifted, :] = placed
                    else:
                        fine_end[c, p, rows, :] = placed
                        fine_end[3 + c, p, rows, :] = moved
            if step + 1 < FINE:
                for p in range(2):
                    send_chunk(step + 1, p, block)
            return carry

        lax.fori_loop(0, blocks, body, 0)

    def share_fine():
        for k in range(1, windows):
            share(fine_end, fines, fine_send, fine_recv, k).start()

    @pl.when(win <= 1)
    def _():
        share_fine()

    fines[win] = fine_end[:, :, own_rows, :]
    starts[win] = states[:, :, own_rows, :]

    @pl.when(win == 0)
    def _():
        out[0] = fine_end[...]

    for side in range(2):

        @pl.when(has_slab[side])
        def _(side=side):
            zone_copy(1 - side).wait_recv()
            material(next_zones[side], 3 * side)

    centre = pl.ds(PAD, part)
    deep = 2

    def wide_copies(n, step):
        a, b = step
        which = around.index(step)
        if b == 0:
            sources = (wide_disp.at[n, :, pl.ds(2, 2), centre, :],)
            sources += (wide_speed.at[n, :, pl.ds(1 + (a + 1) // 2, 1), centre, :],)
            targets = (wide_disp.at[n, :, pl.ds(2 - 2 * a, 2), centre, :],)
            targets += (wide_speed.at[n, :, pl.ds(0 if a > 0 else 3, 1), centre, :],)
        else:
            planes = pl.ds(0, 2) if a == 0 else pl.ds((a + 1) // 2, 1)
            mirror = around.index((-a, -b))
            edge_rows = rim_out.at[n, (b + 1) // 2]
            landing = rim_in.at[n, mirror]
            sources = (edge_rows.at[pl.ds(0, 3)], edge_rows.at[pl.ds(3, 3), planes])
            targets = (landing.at[pl.ds(0, 3)], landing.at[pl.ds(3, 3), planes])
        came = around.index((-a, -b))
        return [
            pltpu.make_async_remote_copy(
                src_ref=source,
                dst_ref=target,
                send_sem=wide_send.at[n, which, k],
                recv_sem=wide_recv.at[n, came, k],
                device_id={"win": win + b, "slab": slab + a},
                device_id_type=MESH,
            )
            for k, (source, target) in enumerate(zip(sources, targets))
        ]

    def turn(n, carry):
        @pl.when(jnp.logical_and(n == 1, win != 0))
        def _():
            shared(fines, fine_recv, 0).wait_recv()

        @pl.when(n != win)
        def _():
            shared(starts, start_recv, n).wait_recv()

        previous = ends.at[n - 1]

        @pl.when(n == 1)
        def _():
            ends[0] = fines[0]

        for c in range(3):
            for p in range(2):
                gap = previous[c, p] - starts[n, c, p]
                gap_speed = previous[3 + c, p] - starts[n, 3 + c, p]
                wide_disp[n, c, 2 + p, centre, :] = gap
                wide_speed[n, c, 1 + p, centre, :] = gap_speed
                for side in range(2):
                    first = (part - deep) * side
                    rim_out[n, side, c, p] = gap[first : first + deep]
                    rim_out[n, side, 3 + c, p] = gap_speed[first : first + deep]
        for step in around:

            @pl.when(present(step))
            def _(step=step):
                for copy in wide_copies(n, step):
                    copy.start()

        @pl.when(win == n + 1)
        def _():
            share_fine()

        for step in around:

            @pl.when(present(step))
            def _(step=step):
                a, b = step
                for copy in wide_copies(n, (-a, -b)):
                    copy.wait_recv()
                if b:
                    which = around.index(step)
                    rows = pl.ds(PAD - deep if b < 0 else PAD + part, deep)
                    for c in range(3):
                        for p in range(2):
                            wide_disp[n, c, 2 + 2 * a + p, rows, :] = rim_in[n, which, c, p]
                        for p in range(2) if a == 0 else ((1 if a < 0 else 0),):
                            q = 1 + 2 * a + p
                            wide_speed[n, c, q, rows, :] = rim_in[n, which, 3 + c, p]

        rows = pl.ds(pl.multiple_of(win * part, 8), wide)
        for q in range(4):
            planes = [[wide_disp[n, c, q + k] for c in range(3)] for k in range(3)]
            laps, leads = stencil(*planes, 0)
            mu = shear[q, rows, :]
            stiff = bulk[q, rows, :]
            for c in range(3):
                rate = mu * laps[c] + stiff * leads[c]
                moved = wide_speed[n, c, q] + DT_COARSE * rate
                mid_disp[c, q] = planes[1][c] + DT_COARSE * moved
                if q in (1, 2):
                    mid_speed[c, q - 1] = moved[PAD : PAD + part]

        @pl.when(n != win)
        def _():
            shared(fines, fine_recv, n).wait_recv()

        rows = pl.ds(pl.multiple_of(win * part + PAD, 8), part)
        for p in range(2):
            planes = [[mid_disp[c, p + k] for c in range(3)] for k in range(3)]
            laps, leads = stencil(*planes, PAD)
            mu = shear[1 + p, rows, :]
            stiff = bulk[1 + p, rows, :]
            for c in range(3):
                rate = mu * laps[c] + stiff * leads[c]
                moved = mid_speed[c, p] + DT_COARSE * rate
                placed = planes[1][c][PAD : PAD + part] + DT_COARSE * moved
                ends[n, c, p] = fines[n, c, p] + placed
                ends[n, 3 + c, p] = fines[n, 3 + c, p] + moved

        @pl.when(n == win)
        def _():
            out[0, :, :, own_rows, :] = ends[n]

        @pl.when(n != win)
        def _():
            home(n).start()

        for step in around:

            @pl.when(present(step))
            def _(step=step):
                for copy in wide_copies(n, step):
                    copy.wait_send()

        return carry

    def home(n):
        return pltpu.make_async_remote_copy(
            src_ref=ends.at[n],
            dst_ref=out.at[0, :, :, own_rows, :],
            send_sem=home_send.at[n],
            recv_sem=home_recv.at[win],
            device_id={"win": n},
            device_id_type=MESH,
        )

    lax.fori_loop(1, windows, turn, 0)

    for n in range(windows):

        if n:

            @pl.when(n != win)
            def _(n=n):
                home(n).wait_send()

        @pl.when(jnp.logical_and(win != 0, n != win))
        def _(n=n):
            rows = pl.ds(n * part, part)
            pltpu.make_async_remote_copy(
                src_ref=ends.at[0],
                dst_ref=out.at[0, :, :, rows, :],
                send_sem=home_send.at[0],
                recv_sem=home_recv.at[n],
                device_id={"win": lax.rem(win + 1, windows)},
                device_id_type=MESH,
            ).wait_recv()

    for k in range(1, windows):

        @pl.when(win != 0)
        def _(k=k):
            share(states, starts, start_send, start_recv, k).wait_send()

        share(fine_end, fines, fine_send, fine_recv, k).wait_send()
    for p in range(2):

        @pl.when(has_slab[p])
        def _(p=p):
            zone_copy(p).wait_send()
            for slot in range(FINE):
                for block in range(blocks):
                    halo_copy(slot, p, block).wait_send()


def solution(mesh):
    windows, slabs = mesh.shape["win"], mesh.shape["slab"]

    def shards(states, load, zones, shear_table, lame_table, amp_table, cycle_index):
        _, _, nz, ny, nx = states.shape
        f32 = jnp.float32
        tall = ny + 2 * PAD
        part = ny // windows
        wide = part + 2 * PAD
        dma = pltpu.SemaphoreType.DMA
        return pl.pallas_call(
            lambda *refs: kernel(windows, slabs, *refs),
            out_shape=jax.ShapeDtypeStruct(states.shape, f32),
            in_specs=[pl.BlockSpec(memory_space=pl.ANY)] * 7,
            out_specs=pl.BlockSpec(memory_space=pltpu.VMEM),
            scratch_shapes=[
                pltpu.VMEM(states.shape[1:], f32),
                pltpu.VMEM(load.shape, load.dtype),
                pltpu.VMEM(zones.shape, jnp.int32),
                pltpu.SMEM(shear_table.shape, f32),
                pltpu.SMEM(lame_table.shape, f32),
                pltpu.SMEM(amp_table.shape, f32),
                pltpu.SMEM(cycle_index.shape, jnp.int32),
                pltpu.VMEM((FINE, 3, nz, tall, nx), f32),
                pltpu.VMEM((FINE, 2, 3, tall, nx), f32),
                pltpu.VMEM((3, nz, ny, nx), f32),
                pltpu.VMEM((6, nz, ny, nx), f32),
                pltpu.VMEM((2, ny, nx), jnp.int32),
                pltpu.VMEM((4, tall, nx), f32),
                pltpu.VMEM((4, tall, nx), f32),
                pltpu.VMEM((windows, 6, nz, part, nx), f32),
                pltpu.VMEM((windows, 6, nz, part, nx), f32),
                pltpu.VMEM((windows, 6, nz, part, nx), f32),
                pltpu.VMEM((windows, 3, 6, wide, nx), f32),
                pltpu.VMEM((windows, 3, 4, wide, nx), f32),
                pltpu.VMEM((3, 4, wide, nx), f32),
                pltpu.VMEM((3, 2, part, nx), f32),
                pltpu.VMEM((windows, 2, 6, 2, 2, nx), f32),
                pltpu.VMEM((windows, 8, 6, 2, 2, nx), f32),
                dma((7,)),
                dma((2,)),
                dma((2,)),
                dma((FINE, 2, ny // ROWS)),
                dma((FINE, 2, ny // ROWS)),
                dma((windows,)),
                dma((windows,)),
                dma((windows,)),
                dma((windows,)),
                dma((windows,)),
                dma((windows,)),
                dma((windows, 8, 2)),
                dma((windows, 8, 2)),
            ],
            compiler_params=pltpu.CompilerParams(
                collective_id=0, has_side_effects=True, vmem_limit_bytes=60 * 2**20
            ),
            name="parareal",
        )(states, load, zones, shear_table, lame_table, amp_table, cycle_index)

    placed = (
        P("win", None, "slab", None, None),
        P(None, "slab", None, None),
        P("slab", None, None),
        P(),
        P(),
        P(),
        P(),
    )
    return jax.shard_map(
        shards,
        mesh=mesh,
        in_specs=placed,
        out_specs=P("win", None, "slab", None, None),
        check_vma=False,
    )
```

```python
import jax
import jax.numpy as jnp
from jax import lax
from jax.experimental import pallas as pl
from jax.experimental.pallas import tpu as pltpu
from jax.sharding import PartitionSpec as P

FINE = 4
DT_FINE = 0.18
DT_COARSE = 0.36
PAD = 8
ROWS = 32
MESH = pl.DeviceIdType.MESH


def stencil(low, mid, high, trim):
    tall, nx = mid[0].shape
    size = tall - 2 * trim
    lane = lax.broadcasted_iota(jnp.int32, (size, nx), 1)
    first_lane = lane == 0
    last_lane = lane == nx - 1

    def left(f):
        return jnp.where(first_lane, 0.0, pltpu.roll(f, 1, 1))

    def right(f):
        return jnp.where(last_lane, 0.0, pltpu.roll(f, nx - 1, 1))

    def core(f):
        return f[trim : trim + size]

    def above(f):
        return core(pltpu.roll(f, 1, 0))

    def below(f):
        return core(pltpu.roll(f, tall - 1, 0))

    zs = [low[c] + high[c] for c in range(3)]
    zd = [high[c] - low[c] for c in range(3)]
    laps = []
    for c in range(3):
        face = 3.0 * zs[c] + 14.0 * mid[c]
        diag = zs[c] + 3.0 * mid[c]
        side = core(face) + above(diag) + below(diag)
        laps.append(
            14.0 * core(zs[c])
            - 128.0 * core(mid[c])
            + (above(face) + below(face))
            + (left(side) + right(side))
        )
    ux, uy = mid[0], mid[1]
    uy_up, uy_down = below(uy), above(uy)
    cross = (uy_up - uy_down) + core(zd[2])
    ux_core = core(ux)
    lead_x = (left(ux_core) + right(ux_core) - 2.0 * ux_core) + 0.25 * (right(cross) - left(cross))
    row_diff = below(ux) - above(ux)
    lead_y = (uy_up + uy_down - 2.0 * core(uy)) + 0.25 * (
        (right(row_diff) - left(row_diff)) + (below(zd[2]) - above(zd[2]))
    )
    zx = core(zd[0])
    lead_z = (core(zs[2]) - 2.0 * core(mid[2])) + 0.25 * (
        (right(zx) - left(zx)) + (below(zd[1]) - above(zd[1]))
    )
    return laps, (lead_x, lead_y, lead_z)


def kernel(
    windows,
    slabs,
    states_hbm,
    load_hbm,
    zones_hbm,
    shear_hbm,
    lame_hbm,
    amp_hbm,
    cycle_hbm,
    out,
    states,
    load,
    zones,
    shear_table,
    lame_table,
    amp_table,
    cycle_index,
    disp,
    halo,
    speed,
    fine_end,
    next_zones,
    shear,
    bulk,
    starts,
    fines,
    ends,
    wide_disp,
    wide_speed,
    mid_disp,
    mid_speed,
    rim_out,
    rim_in,
    load_sem,
    zone_send,
    zone_recv,
    halo_send,
    halo_recv,
    start_send,
    start_recv,
    fine_send,
    fine_recv,
    home_send,
    home_recv,
    wide_send,
    wide_recv,
):
    win = lax.axis_index("win")
    slab = lax.axis_index("slab")
    ny, nx = states.shape[2], states.shape[3]
    part = ny // windows
    wide = part + 2 * PAD
    inner = pl.ds(PAD, ny)
    own_rows = pl.ds(pl.multiple_of(win * part, 8), part)
    has_slab = (slab > 0, slab < slabs - 1)
    has_win = (win > 0, win < windows - 1)

    pairs = (
        (states_hbm.at[0], states),
        (zones_hbm, zones),
        (load_hbm, load),
        (shear_hbm, shear_table),
        (lame_hbm, lame_table),
        (amp_hbm, amp_table),
        (cycle_hbm, cycle_index),
    )
    loads = [pltpu.make_async_copy(a, b, load_sem.at[k]) for k, (a, b) in enumerate(pairs)]
    for copy in loads:
        copy.start()

    around = [(a, b) for a in (-1, 0, 1) for b in (-1, 0, 1) if (a, b) != (0, 0)]

    def present(step):
        a, b = step
        found = None
        if a:
            found = has_slab[(a + 1) // 2]
        if b:
            side = has_win[(b + 1) // 2]
            found = side if found is None else jnp.logical_and(found, side)
        return found

    barrier = pltpu.get_barrier_semaphore()
    expected = jnp.int32(windows - 1)
    for k in range(1, windows):
        target = {"win": lax.rem(win + k, windows)}
        pl.semaphore_signal(barrier, inc=1, device_id=target, device_id_type=MESH)
    for a, b in around:
        if a:
            there = present((a, b))
            expected = expected + there.astype(jnp.int32)

            @pl.when(there)
            def _(a=a, b=b):
                target = {"win": win + b, "slab": slab + a}
                pl.semaphore_signal(barrier, inc=1, device_id=target, device_id_type=MESH)

    edge = jnp.zeros((PAD, nx), jnp.float32)
    for c in range(3):
        for slot in range(disp.shape[0]):
            for p in range(2):
                disp[slot, c, p, pl.ds(0, PAD), :] = edge
                disp[slot, c, p, pl.ds(PAD + ny, PAD), :] = edge
        for slot in range(halo.shape[0]):
            for side in range(2):
                halo[slot, side, c, pl.ds(0, PAD), :] = edge
                halo[slot, side, c, pl.ds(PAD + ny, PAD), :] = edge
    plane_zero = jnp.zeros((ny, nx), jnp.float32)
    for side in range(2):

        @pl.when(jnp.logical_not(has_slab[side]))
        def _(side=side):
            for slot in range(halo.shape[0]):
                for c in range(3):
                    halo[slot, side, c, inner, :] = plane_zero

    def clear(n, carry):
        for c in range(3):
            wide_disp[n, c] = jnp.zeros(wide_disp.shape[2:], jnp.float32)
            wide_speed[n, c] = jnp.zeros(wide_speed.shape[2:], jnp.float32)
        return carry

    lax.fori_loop(0, wide_disp.shape[0], clear, 0)
    tall_zero = jnp.zeros(shear.shape[1:], jnp.float32)
    for q in range(4):
        shear[q] = tall_zero
        bulk[q] = tall_zero

    pl.semaphore_wait(barrier, expected)

    blocks = ny // ROWS

    def halo_copy(slot, p, block):
        start = pl.multiple_of(block * ROWS, ROWS)
        shifted = pl.ds(start + PAD, ROWS)
        if slot == 0:
            source = states.at[pl.ds(0, 3), p, pl.ds(start, ROWS), :]
        else:
            source = disp.at[slot, :, p, shifted, :]
        return pltpu.make_async_remote_copy(
            src_ref=source,
            dst_ref=halo.at[slot, 1 - p, :, shifted, :],
            send_sem=halo_send.at[slot, p, block],
            recv_sem=halo_recv.at[slot, 1 - p, block],
            device_id={"slab": slab - 1 + 2 * p},
            device_id_type=MESH,
        )

    def send_chunk(slot, p, block):
        @pl.when(has_slab[p])
        def _():
            halo_copy(slot, p, block).start()

    def await_chunk(slot, block):
        for side in range(2):

            @pl.when(has_slab[side])
            def _(side=side):
                halo_copy(slot, 1 - side, block).wait_recv()

    def zone_copy(p):
        return pltpu.make_async_remote_copy(
            src_ref=zones.at[p],
            dst_ref=next_zones.at[1 - p],
            send_sem=zone_send.at[p],
            recv_sem=zone_recv.at[1 - p],
            device_id={"slab": slab - 1 + 2 * p},
            device_id_type=MESH,
        )

    def share(source, target, send, recv, k):
        other = lax.rem(win + k, windows)
        return pltpu.make_async_remote_copy(
            src_ref=source.at[:, :, pl.ds(pl.multiple_of(other * part, 8), part), :],
            dst_ref=target.at[win],
            send_sem=send.at[k],
            recv_sem=recv.at[win],
            device_id={"win": other},
            device_id_type=MESH,
        )

    def shared(target, recv, n):
        return pltpu.make_async_remote_copy(
            src_ref=target.at[n],
            dst_ref=target.at[n],
            send_sem=recv.at[n],
            recv_sem=recv.at[n],
            device_id={"win": lax.rem(win + 1, windows)},
            device_id_type=MESH,
        )

    loads[0].wait()
    for block in range(blocks):
        for p in range(2):
            send_chunk(0, p, block)
    loads[1].wait()
    for p in range(2):

        @pl.when(has_slab[p])
        def _(p=p):
            zone_copy(p).start()

    for c in range(3):
        for p in range(2):
            disp[0, c, p, inner, :] = states[c, p]
            speed[c, p] = states[3 + c, p]
    for copy in loads[2:]:
        copy.wait()

    def material(ids, q):
        mu = jnp.zeros(ids.shape, jnp.float32)
        lame = jnp.zeros(ids.shape, jnp.float32)
        for k in range(shear_table.shape[0]):
            mu = jnp.where(ids == k, shear_table[k], mu)
            lame = jnp.where(ids == k, lame_table[k], lame)
        shear[q, inner, :] = mu * (1.0 / 30.0)
        bulk[q, inner, :] = lame + mu

    for p in range(2):
        material(zones[p], 1 + p)
    amp = amp_table[cycle_index[win]]

    for step in range(FINE):

        @pl.when((win + 1) // 2 == step + 1)
        def _():
            for k in range(1, windows):
                share(states, starts, start_send, start_recv, k).start()

        await_chunk(step, 0)

        def body(block, carry, step=step):
            @pl.when(block + 1 < blocks)
            def _():
                await_chunk(step, block + 1)

            start = pl.multiple_of(block * ROWS, ROWS)
            rows = pl.ds(start, ROWS)
            shifted = pl.ds(start + PAD, ROWS)
            window = pl.ds(start, ROWS + 2 * PAD)
            for p in range(2):
                low, mid, high = [], [], []
                for c in range(3):
                    own = [disp[step, c, q, window, :] for q in range(2)]
                    mid.append(own[p])
                    low.append(halo[step, 0, c, window, :] if p == 0 else own[0])
                    high.append(own[1] if p == 0 else halo[step, 1, c, window, :])
                laps, leads = stencil(low, mid, high, PAD)
                mu = shear[1 + p, shifted, :]
                stiff = bulk[1 + p, shifted, :]
                for c in range(3):
                    rate = mu * laps[c] + stiff * leads[c]
                    rate = rate + amp * load[c, p, rows, :].astype(jnp.float32)
                    moved = speed[c, p, rows, :] + DT_FINE * rate
                    placed = mid[c][PAD : PAD + ROWS] + DT_FINE * moved
                    if step + 1 < FINE:
                        speed[c, p, rows, :] = moved
                        disp[step + 1, c, p, shifted, :] = placed
                    else:
                        fine_end[c, p, rows, :] = placed
                        fine_end[3 + c, p, rows, :] = moved
            if step + 1 < FINE:
                for p in range(2):
                    send_chunk(step + 1, p, block)
            return carry

        lax.fori_loop(0, blocks, body, 0)

    def share_fine():
        for k in range(1, windows):
            share(fine_end, fines, fine_send, fine_recv, k).start()

    share_fine()

    fines[win] = fine_end[:, :, own_rows, :]
    starts[win] = states[:, :, own_rows, :]

    @pl.when(win == 0)
    def _():
        out[0] = fine_end[...]

    for side in range(2):

        @pl.when(has_slab[side])
        def _(side=side):
            zone_copy(1 - side).wait_recv()
            material(next_zones[side], 3 * side)

    centre = pl.ds(PAD, part)
    deep = 2

    def wide_copies(n, step):
        a, b = step
        which = around.index(step)
        if b == 0:
            sources = (wide_disp.at[n, :, pl.ds(2, 2), centre, :],)
            sources += (wide_speed.at[n, :, pl.ds(1 + (a + 1) // 2, 1), centre, :],)
            targets = (wide_disp.at[n, :, pl.ds(2 - 2 * a, 2), centre, :],)
            targets += (wide_speed.at[n, :, pl.ds(0 if a > 0 else 3, 1), centre, :],)
        else:
            planes = pl.ds(0, 2) if a == 0 else pl.ds((a + 1) // 2, 1)
            mirror = around.index((-a, -b))
            edge_rows = rim_out.at[n, (b + 1) // 2]
            landing = rim_in.at[n, mirror]
            sources = (edge_rows.at[pl.ds(0, 3)], edge_rows.at[pl.ds(3, 3), planes])
            targets = (landing.at[pl.ds(0, 3)], landing.at[pl.ds(3, 3), planes])
        came = around.index((-a, -b))
        return [
            pltpu.make_async_remote_copy(
                src_ref=source,
                dst_ref=target,
                send_sem=wide_send.at[n, which, k],
                recv_sem=wide_recv.at[n, came, k],
                device_id={"win": win + b, "slab": slab + a},
                device_id_type=MESH,
            )
            for k, (source, target) in enumerate(zip(sources, targets))
        ]

    def turn(n, carry):
        @pl.when(jnp.logical_and(n == 1, win != 0))
        def _():
            shared(fines, fine_recv, 0).wait_recv()

        @pl.when(n != win)
        def _():
            shared(starts, start_recv, n).wait_recv()

        previous = ends.at[n - 1]

        @pl.when(n == 1)
        def _():
            ends[0] = fines[0]

        for c in range(3):
            for p in range(2):
                gap = previous[c, p] - starts[n, c, p]
                gap_speed = previous[3 + c, p] - starts[n, 3 + c, p]
                wide_disp[n, c, 2 + p, centre, :] = gap
                wide_speed[n, c, 1 + p, centre, :] = gap_speed
                for side in range(2):
                    first = (part - deep) * side
                    rim_out[n, side, c, p] = gap[first : first + deep]
                    rim_out[n, side, 3 + c, p] = gap_speed[first : first + deep]
        for step in around:

            @pl.when(present(step))
            def _(step=step):
                for copy in wide_copies(n, step):
                    copy.start()

        for step in around:

            @pl.when(present(step))
            def _(step=step):
                a, b = step
                for copy in wide_copies(n, (-a, -b)):
                    copy.wait_recv()
                if b:
                    which = around.index(step)
                    rows = pl.ds(PAD - deep if b < 0 else PAD + part, deep)
                    for c in range(3):
                        for p in range(2):
                            wide_disp[n, c, 2 + 2 * a + p, rows, :] = rim_in[n, which, c, p]
                        for p in range(2) if a == 0 else ((1 if a < 0 else 0),):
                            q = 1 + 2 * a + p
                            wide_speed[n, c, q, rows, :] = rim_in[n, which, 3 + c, p]

        rows = pl.ds(pl.multiple_of(win * part, 8), wide)
        for q in range(4):
            planes = [[wide_disp[n, c, q + k] for c in range(3)] for k in range(3)]
            laps, leads = stencil(*planes, 0)
            mu = shear[q, rows, :]
            stiff = bulk[q, rows, :]
            for c in range(3):
                rate = mu * laps[c] + stiff * leads[c]
                moved = wide_speed[n, c, q] + DT_COARSE * rate
                mid_disp[c, q] = planes[1][c] + DT_COARSE * moved
                if q in (1, 2):
                    mid_speed[c, q - 1] = moved[PAD : PAD + part]

        @pl.when(n != win)
        def _():
            shared(fines, fine_recv, n).wait_recv()

        rows = pl.ds(pl.multiple_of(win * part + PAD, 8), part)
        for p in range(2):
            planes = [[mid_disp[c, p + k] for c in range(3)] for k in range(3)]
            laps, leads = stencil(*planes, PAD)
            mu = shear[1 + p, rows, :]
            stiff = bulk[1 + p, rows, :]
            for c in range(3):
                rate = mu * laps[c] + stiff * leads[c]
                moved = mid_speed[c, p] + DT_COARSE * rate
                placed = planes[1][c][PAD : PAD + part] + DT_COARSE * moved
                ends[n, c, p] = fines[n, c, p] + placed
                ends[n, 3 + c, p] = fines[n, 3 + c, p] + moved

        @pl.when(n == win)
        def _():
            out[0, :, :, own_rows, :] = ends[n]

        @pl.when(n != win)
        def _():
            home(n).start()

        for step in around:

            @pl.when(present(step))
            def _(step=step):
                for copy in wide_copies(n, step):
                    copy.wait_send()

        return carry

    def home(n):
        return pltpu.make_async_remote_copy(
            src_ref=ends.at[n],
            dst_ref=out.at[0, :, :, own_rows, :],
            send_sem=home_send.at[n],
            recv_sem=home_recv.at[win],
            device_id={"win": n},
            device_id_type=MESH,
        )

    lax.fori_loop(1, windows, turn, 0)

    for n in range(windows):

        if n:

            @pl.when(n != win)
            def _(n=n):
                home(n).wait_send()

        @pl.when(jnp.logical_and(win != 0, n != win))
        def _(n=n):
            rows = pl.ds(n * part, part)
            pltpu.make_async_remote_copy(
                src_ref=ends.at[0],
                dst_ref=out.at[0, :, :, rows, :],
                send_sem=home_send.at[0],
                recv_sem=home_recv.at[n],
                device_id={"win": lax.rem(win + 1, windows)},
                device_id_type=MESH,
            ).wait_recv()

    for k in range(1, windows):

        @pl.when(win != 0)
        def _(k=k):
            share(states, starts, start_send, start_recv, k).wait_send()

        share(fine_end, fines, fine_send, fine_recv, k).wait_send()
    for p in range(2):

        @pl.when(has_slab[p])
        def _(p=p):
            zone_copy(p).wait_send()
            for slot in range(FINE):
                for block in range(blocks):
                    halo_copy(slot, p, block).wait_send()


def solution(mesh):
    windows, slabs = mesh.shape["win"], mesh.shape["slab"]

    def shards(states, load, zones, shear_table, lame_table, amp_table, cycle_index):
        _, _, nz, ny, nx = states.shape
        f32 = jnp.float32
        tall = ny + 2 * PAD
        part = ny // windows
        wide = part + 2 * PAD
        dma = pltpu.SemaphoreType.DMA
        return pl.pallas_call(
            lambda *refs: kernel(windows, slabs, *refs),
            out_shape=jax.ShapeDtypeStruct(states.shape, f32),
            in_specs=[pl.BlockSpec(memory_space=pl.ANY)] * 7,
            out_specs=pl.BlockSpec(memory_space=pltpu.VMEM),
            scratch_shapes=[
                pltpu.VMEM(states.shape[1:], f32),
                pltpu.VMEM(load.shape, load.dtype),
                pltpu.VMEM(zones.shape, jnp.int32),
                pltpu.SMEM(shear_table.shape, f32),
                pltpu.SMEM(lame_table.shape, f32),
                pltpu.SMEM(amp_table.shape, f32),
                pltpu.SMEM(cycle_index.shape, jnp.int32),
                pltpu.VMEM((FINE, 3, nz, tall, nx), f32),
                pltpu.VMEM((FINE, 2, 3, tall, nx), f32),
                pltpu.VMEM((3, nz, ny, nx), f32),
                pltpu.VMEM((6, nz, ny, nx), f32),
                pltpu.VMEM((2, ny, nx), jnp.int32),
                pltpu.VMEM((4, tall, nx), f32),
                pltpu.VMEM((4, tall, nx), f32),
                pltpu.VMEM((windows, 6, nz, part, nx), f32),
                pltpu.VMEM((windows, 6, nz, part, nx), f32),
                pltpu.VMEM((windows, 6, nz, part, nx), f32),
                pltpu.VMEM((windows, 3, 6, wide, nx), f32),
                pltpu.VMEM((windows, 3, 4, wide, nx), f32),
                pltpu.VMEM((3, 4, wide, nx), f32),
                pltpu.VMEM((3, 2, part, nx), f32),
                pltpu.VMEM((windows, 2, 6, 2, 2, nx), f32),
                pltpu.VMEM((windows, 8, 6, 2, 2, nx), f32),
                dma((7,)),
                dma((2,)),
                dma((2,)),
                dma((FINE, 2, ny // ROWS)),
                dma((FINE, 2, ny // ROWS)),
                dma((windows,)),
                dma((windows,)),
                dma((windows,)),
                dma((windows,)),
                dma((windows,)),
                dma((windows,)),
                dma((windows, 8, 2)),
                dma((windows, 8, 2)),
            ],
            compiler_params=pltpu.CompilerParams(
                collective_id=0, has_side_effects=True, vmem_limit_bytes=60 * 2**20
            ),
            name="parareal",
        )(states, load, zones, shear_table, lame_table, amp_table, cycle_index)

    placed = (
        P("win", None, "slab", None, None),
        P(None, "slab", None, None),
        P("slab", None, None),
        P(),
        P(),
        P(),
        P(),
    )
    return jax.shard_map(
        shards,
        mesh=mesh,
        in_specs=placed,
        out_specs=P("win", None, "slab", None, None),
        check_vma=False,
    )
```
